32 devices in a mesh: groups: 2 (over x), gx: 16 (over z, y, core).
Axes of the slice: x: 2, y: 2, z: 4, core: 2. Of those that a mesh axis runs over, the one named last changes fastest.
Arguments:
- positions: float32 [3, 131072], P(None, ('groups', 'gx')), parts along dimension 1, may hold values from -0.08 to 127.08, as said below
- radii: float32 [131072], P(('groups', 'gx')), parts along dimension 0, may hold values from 0.5 to 0.56
- neighbours: int32 [6, 131072], P(None, ('groups', 'gx')), parts along dimension 1, may hold values from 0 to 65535, as said below
- right_side: float32 [3, 131072], P(None, ('groups', 'gx')), parts along dimension 1, may hold values from -6 to 6
Outputs:
- solution_field: float32 [3, 131072], P(None, ('groups', 'gx')), parts along dimension 1
- residual: float32 [3, 131072], P(None, ('groups', 'gx')), parts along dimension 1
The draws below stay inside these ranges and needn't reach their ends.
There are 2 independent parts, one for each index of `groups`. The reference program is written for one: setup_inputs(seed, part) draws one part's arguments, and reference() takes and returns one part's arrays. A program takes and returns all parts, laid end to end along the dimension named above; each array names one. Nothing has to cross between parts.
Inputs may be any that keep to these rules, and one draw needn't show every extreme that they name: `positions`: particles are ordered by lattice planes of 2048 along the first coordinate, rows of 128 within a plane; each lies within 0.08 of its lattice site in every coordinate. `neighbours`: each column lists distinct partners of the particle, the other slots hold the particle's own index; partnership is symmetric; every partner index is the particle's index plus or minus 1, 128 or 2048.
All inputs are finite; a program needn't handle non-finite values.
Results may differ from the reference program's by a relative error of at most 0.0003.
Values sent between devices are 32-bit elements; how exact they have to be, the bound alone decides.
A program may use at most 64 MiB of HBM per device.

```python
import jax
import jax.numpy as jnp
from jax import lax

LY = 16
LZ = 128
ITERS = 4
LX = 32
PARTICLES = 65536


def lattice_sites():
    particle_ids = jnp.arange(PARTICLES, dtype=jnp.int32)
    first = particle_ids // (LY * LZ)
    second = particle_ids // LZ % LY
    third = particle_ids % LZ
    return (particle_ids, first, second, third)


def draw_positions(key, part):
    particle_ids, first, second, third = lattice_sites()
    sites = jnp.stack([first, second, third], axis=0).astype(jnp.float32)
    jitter = jnp.clip(0.03 * jax.random.normal(key, (3, PARTICLES), jnp.float32), -0.08, 0.08)
    return sites + jitter


def draw_neighbours(key, part):
    particle_ids, first, second, third = lattice_sites()
    plane_size = LY * LZ
    bonds = jax.random.randint(jax.random.fold_in(key, 11), (3, PARTICLES), 0, 5) > 0
    bond_first = bonds[0] & (first < LX - 1)
    bond_second = bonds[1] & (second < LY - 1)
    bond_third = bonds[2] & (third < LZ - 1)
    back_first = jnp.roll(bond_first, plane_size) & (first > 0)
    back_second = jnp.roll(bond_second, LZ) & (second > 0)
    back_third = jnp.roll(bond_third, 1) & (third > 0)
    slots = jnp.stack([jnp.where(bond_first, particle_ids + plane_size, particle_ids), jnp.where(back_first, particle_ids - plane_size, particle_ids), jnp.where(bond_second, particle_ids + LZ, particle_ids), jnp.where(back_second, particle_ids - LZ, particle_ids), jnp.where(bond_third, particle_ids + 1, particle_ids), jnp.where(back_third, particle_ids - 1, particle_ids)], axis=0)
    scores = jax.random.randint(jax.random.fold_in(key, 12), (6, PARTICLES), 0, 1048576) * 8
    scores = scores + jnp.arange(6, dtype=jnp.int32)[:, None]
    order = jnp.argsort(scores, axis=0)
    return jnp.take_along_axis(slots, order, axis=0).astype(jnp.int32)


def draw_right_side(key, part):
    particle_ids, first, second, third = lattice_sites()
    ramp = 0.5 + first.astype(jnp.float32) / (LX - 1)
    values = jnp.clip(jax.random.normal(key, (3, PARTICLES), jnp.float32), -4.0, 4.0) * ramp[None, :]
    return values.astype(jnp.float32)


def levels(stream_key, extent, cuts, least, top_value):
    level = 1.0
    for position, shards_of in cuts:
        heights = jax.random.uniform(jax.random.fold_in(jax.random.fold_in(stream_key, 6), position), (shards_of,), jnp.float32, least / len(cuts), top_value / len(cuts))
        level = level * jnp.repeat(jnp.exp(heights), extent[position] // shards_of).reshape((-1,) + (1,) * (len(extent) - 1 - position))
    return level


def setup_inputs(seed: int = 0, part: int = 0) -> dict:
    keys = jax.random.split(jax.random.key(seed), 5)
    own_keys = jax.random.split(jax.random.fold_in(keys[4], part), 5)
    positions = draw_positions(jax.random.fold_in(jax.random.fold_in(keys[4], part), 71), part)
    radii = jnp.clip(0.5 + 0.060000002 * jax.random.uniform(own_keys[1], (PARTICLES,), jnp.float32) ** levels(own_keys[1], (PARTICLES,), ((0, 16),), -0.2, 0.2), 0.5, 0.56)
    neighbours = draw_neighbours(jax.random.fold_in(jax.random.fold_in(keys[4], part), 71), part)
    right_side = draw_right_side(jax.random.fold_in(jax.random.fold_in(keys[4], part), 71), part)
    return dict(positions=positions, radii=radii, neighbours=neighbours, right_side=right_side)


diagonal_shift = 4.0

def pair_terms(own_geom, ext_geom, local_index, present):
    partner = jnp.take(ext_geom[:3], local_index, axis=1)
    offset = partner - own_geom[:3][:, None, :]
    squared = lax.optimization_barrier(jnp.sum(offset * offset, axis=0))
    distance = jnp.sqrt(jnp.where(present, squared, jnp.float32(1.0)))
    normal = offset / distance
    contact = own_geom[3][None, :] + jnp.take(ext_geom[3], local_index, axis=0)
    stiffness = 1.0 / (contact * contact)
    tension = -(1.0 - distance / contact) / (contact * distance)
    live_mask = present.astype(jnp.float32)
    return (normal, tension * live_mask, (stiffness - tension) * live_mask)

def apply_terms(vector, extended, local_index, blocks):
    normal, tension, radial = blocks
    partner = jnp.take(extended, local_index, axis=1)
    relative = vector[:, None, :] - partner
    along_normal = lax.optimization_barrier(jnp.sum(normal * relative, axis=0))
    return diagonal_shift * vector + lax.optimization_barrier(jnp.sum(tension * relative + radial * normal * along_normal, axis=1))

def reference(positions, radii, neighbours, right_side):
    owned = positions.shape[1]
    particle_ids = jnp.arange(owned, dtype=jnp.int32)
    present = neighbours != particle_ids[None, :]
    geometry = jnp.concatenate([positions, radii[None, :]], axis=0)
    blocks = pair_terms(geometry, geometry, neighbours, present)
    solution_field = jnp.zeros_like(right_side)
    residual = right_side
    direction = right_side
    norm_now = jnp.sum(residual * residual)
    for iteration in range(ITERS):
        image_vec = apply_terms(direction, direction, neighbours, blocks)
        step_size = norm_now / jnp.sum(direction * image_vec)
        solution_field = solution_field + step_size * direction
        residual = residual - step_size * image_vec
        norm_next = jnp.sum(residual * residual)
        direction = residual + norm_next / norm_now * direction
        norm_now = norm_next
    return (solution_field, residual)
```

```python
import jax
import jax.numpy as jnp
from jax import lax
from jax.sharding import PartitionSpec as P

LY = 16
LZ = 128
ITERS = 4


diagonal_shift = 4.0


def with_halo(array, width):
    devices, length = (lax.axis_size("gx"), array.shape[1])
    up = [(i, i + 1) for i in range(devices - 1)]
    down = [(j, i) for i, j in up]
    before = lax.ppermute(array[:, length - width :], "gx", up)
    after = lax.ppermute(array[:, :width], "gx", down)
    return jnp.concatenate([before, array, after], axis=1)


def partners(extended, rows):
    def view(start):
        return extended[:, start : start + rows]

    own = view(LY)
    return [
        view(2 * LY),
        view(0),
        view(LY + 1),
        view(LY - 1),
        jnp.concatenate([own[:, :, 1:], view(LY + 1)[:, :, :1]], axis=2),
        jnp.concatenate([view(LY - 1)[:, :, LZ - 1 :], own[:, :, : LZ - 1]], axis=2),
    ]


def pair_terms(own_geom, partner_geom, present):
    offset = partner_geom[:3] - own_geom[:3]
    squared = jnp.sum(offset * offset, axis=0)
    distance = jnp.sqrt(jnp.where(present, squared, jnp.float32(1.0)))
    normal = jnp.where(present[None], offset, 0.0) / distance
    contact = jnp.where(present, own_geom[3] + partner_geom[3], jnp.float32(1.0))
    stiffness = 1.0 / (contact * contact)
    tension = -(1.0 - distance / contact) / (contact * distance)
    live_mask = present.astype(jnp.float32)
    return (normal, tension * live_mask, (stiffness - tension) * live_mask)


def apply_terms(vector, partner, blocks):
    image = diagonal_shift * vector
    for value, (normal, tension, radial) in zip(partner, blocks):
        relative = vector - value
        along = radial * jnp.sum(normal * relative, axis=0)
        image = image + (tension * relative + normal * along)
    return image


def two_products(residual, image_vec):
    return lax.psum((jnp.sum(residual * residual), jnp.sum(residual * image_vec)), "gx")


def on_device(positions, radii, neighbours, right_side):
    owned = positions.shape[1]
    rows = owned // LZ
    shape = right_side.shape
    first_id = lax.axis_index("gx") * owned
    own_ids = (first_id + jnp.arange(owned, dtype=jnp.int32)).reshape(rows, LZ)
    neighbours = neighbours.reshape(-1, rows, LZ)
    offsets = [LY * LZ, -LY * LZ, LZ, -LZ, 1, -1]
    present = [jnp.any(neighbours == own_ids + by, axis=0) for by in offsets]
    geometry = jnp.concatenate([positions, radii[None, :]], axis=0)
    geometry = geometry.reshape(4, rows, LZ)
    right_side = right_side.reshape(3, rows, LZ)
    joined = with_halo(jnp.concatenate([geometry, right_side], axis=0), LY)
    first = partners(joined, rows)
    blocks = [pair_terms(geometry, f[:4], here) for f, here in zip(first, present)]
    blocks = lax.optimization_barrier(blocks)

    def operate(vector):
        return apply_terms(vector, partners(with_halo(vector, LY), rows), blocks)

    solution_field = jnp.zeros_like(right_side)
    residual = right_side
    image_vec = apply_terms(residual, [f[4:] for f in first], blocks)
    norm_now, product = two_products(residual, image_vec)
    step_size = norm_now / product
    direction = residual
    image_dir = image_vec
    for iteration in range(ITERS):
        solution_field = solution_field + step_size * direction
        residual = residual - step_size * image_dir
        if iteration + 1 < ITERS:
            image_vec = operate(residual)
            norm_next, product = two_products(residual, image_vec)
            beta_ratio = norm_next / norm_now
            step_size = norm_next / (product - beta_ratio * norm_next / step_size)
            direction = residual + beta_ratio * direction
            image_dir = image_vec + beta_ratio * image_dir
            norm_now = norm_next
    return (solution_field.reshape(shape), residual.reshape(shape))


def solution(mesh):
    return jax.shard_map(
        on_device,
        mesh=mesh,
        in_specs=(
            P(None, ("groups", "gx")),
            P(("groups", "gx")),
            P(None, ("groups", "gx")),
            P(None, ("groups", "gx")),
        ),
        out_specs=(P(None, ("groups", "gx")), P(None, ("groups", "gx"))),
        check_vma=False,
    )
```
